32 devices in a mesh: groups: 2 (over x), user: 2 (over core), hist: 8 (over z, y).
Axes of the slice: x: 2, y: 2, z: 4, core: 2. Of those that a mesh axis runs over, the one named last changes fastest.
Arguments:
- item_table: bfloat16 [512, 1024], P('hist')
- item_ids: int32 [4, 512], P(('groups', 'user'), 'hist'), parts along dimension 0, may hold values from 0 to 511
- candidate_counts: int32 [4], P(('groups', 'user')), parts along dimension 0, may hold values from 256 to 512, as said below
- domain_ids: int32 [4, 512], P(('groups', 'user'), 'hist'), parts along dimension 0, may hold values from 0 to 1, as said below
- history_lengths: int32 [4], P(('groups', 'user')), parts along dimension 0, may hold values from 2048 to 4096, as said below
- history_keys: bfloat16 [4, 4096, 1024], P(('groups', 'user'), 'hist'), parts along dimension 0, may hold values from -9 to 9
- history_values: bfloat16 [4, 4096, 1024], P(('groups', 'user'), 'hist'), parts along dimension 0
- w_query: bfloat16 [1024, 1024], replicated, may hold values from -0.1875 to 0.1875
- w_gate: bfloat16 [1024, 1024], replicated, may hold values from -0.1875 to 0.1875
- w_out: bfloat16 [1024, 1024], replicated, may hold values from -0.1875 to 0.1875
- attn_gain: float32 [1024], replicated, may hold values from 0.1 to 1.9
- expert_weights: bfloat16 [2, 2, 1024, 1024], P('user'), may hold values from -0.1875 to 0.1875
Outputs:
- candidate_states: bfloat16 [4, 512, 1024], P(('groups', 'user'), 'hist'), parts along dimension 0
The draws below stay inside these ranges and needn't reach their ends.
There are 2 independent parts, one for each index of `groups`. The reference program is written for one: setup_inputs(seed, part) draws one part's arguments, and reference() takes and returns one part's arrays. A program takes and returns all parts, laid end to end along the dimension named above; an argument that names none is the same for every part. Nothing has to cross between parts.
Inputs may be any that keep to these rules, and one draw needn't show every extreme that they name: `candidate_counts`: slots at or past a user's count are padding; some user has 512. `history_lengths`: positions at or past a user's length are not attended; some user has 4096. `domain_ids`: in each aligned block of 64 slots of a user, at most 48 slots name one domain; in the first block of every user exactly 48 name the same domain.
All inputs are finite; a program needn't handle non-finite values.
Results may differ from the reference program's by a relative error of at most 0.0059.
Values may be sent and summed in bfloat16 or wider, within the bound.
A program may use at most 64 MiB of HBM per device.

```python
import math
import jax
import jax.numpy as jnp
import numpy as np
from jax import lax

D = 1024
H = 8
HIST_DEV = 512
SLOT_DEV = 64
LAYERS = 2
CAP = 48
USERS = 2
EXPERTS = 2
HIST = 4096
SLOTS = 512
ITEMS = 512
N_HIST = 8


def scaled_pattern(key, shape, row_lo, row_hi, col_lo, col_hi):
    key_base, key_rows, key_cols = jax.random.split(key, 3)
    row_shape = shape[:-1] + (1,)
    col_shape = (1,) * (len(shape) - 1) + (shape[-1],)
    row_scale = jnp.exp(jax.random.uniform(key_rows, row_shape, jnp.float32, math.log(row_lo), math.log(row_hi)))
    col_scale = jnp.exp(jax.random.uniform(key_cols, col_shape, jnp.float32, math.log(col_lo), math.log(col_hi)))
    pattern = jax.random.normal(key_base, shape, jnp.float32)
    return pattern * row_scale * col_scale


def draw_item_table(key, part):
    return scaled_pattern(key, (ITEMS, D), 0.5, 2.0, 0.4, 4.0).astype(jnp.bfloat16)


def draw_history_values(key, part):
    return scaled_pattern(key, (USERS, HIST, D), 0.5, 2.0, 0.4, 4.0).astype(jnp.bfloat16)


def draw_candidate_counts(key, part):
    key_level, key_full = jax.random.split(key)
    counts = jax.random.randint(key_level, (USERS,), SLOTS // 2, SLOTS + 1)
    full_user = jax.random.randint(key_full, (), 0, USERS)
    return jnp.where(jnp.arange(USERS) == full_user, SLOTS, counts).astype(jnp.int32)


def draw_history_lengths(key, part):
    key_level, key_full = jax.random.split(key)
    lengths = jax.random.randint(key_level, (USERS,), HIST // 2, HIST + 1)
    full_user = jax.random.randint(key_full, (), 0, USERS)
    return jnp.where(jnp.arange(USERS) == full_user, HIST, lengths).astype(jnp.int32)


def draw_domain_ids(key, part):
    blocks = SLOTS // SLOT_DEV
    key_share, key_order, key_heavy = jax.random.split(key, 3)
    light_share = SLOT_DEV - CAP
    first_share = jax.random.randint(key_share, (USERS, blocks, 1), light_share, CAP + 1)
    heavy_domain = jax.random.randint(key_heavy, (), 0, 2)
    heavy_share = jnp.where(heavy_domain == 0, CAP, light_share)
    first_block = (jnp.arange(blocks, dtype=jnp.int32) == 0)[None, :, None]
    first_share = jnp.where(first_block, heavy_share, first_share)
    random_keys = jax.random.randint(key_order, (USERS, blocks, SLOT_DEV), 0, 1 << 20)
    distinct = random_keys * SLOT_DEV + jnp.arange(SLOT_DEV, dtype=jnp.int32)
    ordering = jnp.argsort(distinct, axis=-1, stable=True)
    position = jnp.argsort(ordering, axis=-1, stable=True)
    labels = jnp.where(position < first_share, 0, 1)
    return labels.reshape(USERS, SLOTS).astype(jnp.int32)


def touch_ends(array, own_key, smallest, top_value):
    spot = [jax.random.randint(jax.random.fold_in(own_key, axis), (), 0, length) for axis, length in enumerate(array.shape)]
    longest = array.shape.index(max(array.shape))
    beside = spot[:longest] + [(spot[longest] + 1) % array.shape[longest]] + spot[longest + 1:]
    return array.at[tuple(spot)].set(smallest).at[tuple(beside)].set(top_value)


def block_levels(rng, shape, cuts, smallest, high):
    loudness = 1.0
    for axis_at, blocks in cuts:
        steps = jax.random.uniform(jax.random.fold_in(jax.random.fold_in(rng, 6), axis_at), (blocks,), jnp.float32, smallest / len(cuts), high / len(cuts))
        loudness = loudness * jnp.repeat(jnp.exp(steps), shape[axis_at] // blocks).reshape((-1,) + (1,) * (len(shape) - 1 - axis_at))
    return loudness


def cumulative_ranks(count, slope):
    loads = [(1 << 20) // math.isqrt(standing ** slope) + 1 for standing in range(1, count + 1)]
    scale = 1 + sum(loads) // (1 << 30)
    return np.cumsum(np.array([max(1, weight // scale) for weight in loads]))


def skewed_ids(stream_key, dims, count, slope):
    listing = cumulative_ranks(count, slope)
    lot = jax.random.randint(jax.random.fold_in(stream_key, 1), dims, 0, int(listing[count - 1]))
    rank = jnp.searchsorted(jnp.asarray(listing, jnp.int32), lot, side="right")
    return jax.random.permutation(jax.random.fold_in(stream_key, 2), count)[rank].astype(jnp.int32)


def bell_draw(rng, extent, spread, limit, cuts=(), kind=jnp.bfloat16):
    values = spread * jax.random.normal(rng, extent, jnp.float32)
    if cuts:
        values = values * block_levels(rng, extent, cuts, -0.22, 0.18)
    return jnp.clip(values, -limit, limit).astype(kind)


def setup_inputs(seed: int = 0, part: int = 0) -> dict:
    key_of = jax.random.split(jax.random.key(seed), 13)
    part_splits = jax.random.split(jax.random.fold_in(key_of[12], part), 13)
    return {
        "item_table": draw_item_table(jax.random.fold_in(key_of[12], 71), part),
        "item_ids": touch_ends(skewed_ids(part_splits[1], (USERS, SLOTS), ITEMS, 2), jax.random.fold_in(part_splits[1], 3), 0, ITEMS - 1).astype(jnp.int32),
        "candidate_counts": draw_candidate_counts(jax.random.fold_in(jax.random.fold_in(key_of[12], part), 71), part),
        "domain_ids": draw_domain_ids(jax.random.fold_in(jax.random.fold_in(key_of[12], part), 71), part),
        "history_lengths": draw_history_lengths(jax.random.fold_in(jax.random.fold_in(key_of[12], part), 71), part),
        "history_keys": bell_draw(part_splits[5], (USERS, HIST, D), 1.5, 9.0, ((0, 2), (1, 8))),
        "history_values": draw_history_values(jax.random.fold_in(jax.random.fold_in(key_of[12], part), 71), part),
        "w_query": bell_draw(key_of[7], (D, D), D ** -0.5, 0.1875),
        "w_gate": bell_draw(key_of[8], (D, D), D ** -0.5, 0.1875),
        "w_out": bell_draw(key_of[9], (D, D), D ** -0.5, 0.1875),
        "attn_gain": jnp.clip(1.0 + 0.18 * jax.random.normal(key_of[10], (D,), jnp.float32), 0.1, 1.9),
        "expert_weights": bell_draw(key_of[11], (EXPERTS, LAYERS, D, D), D ** -0.5, 0.1875, ((0, 2),)),
    }


norm_eps = 1e-05

def rms_scale(matrix):
    return matrix * lax.rsqrt(lax.optimization_barrier(jnp.mean(matrix * matrix, axis=-1, keepdims=True)) + norm_eps)

def attend_local(query_rows, key_rows, value_rows, key_live):
    row_count = query_rows.shape[0]
    feat_width = query_rows.shape[1]
    head_size = feat_width // H
    query_heads = query_rows.astype(jnp.float32).reshape(row_count, H, head_size)
    key_heads = key_rows.astype(jnp.float32).reshape(key_rows.shape[0], H, head_size)
    value_heads = value_rows.astype(jnp.float32).reshape(value_rows.shape[0], H, head_size)
    scores = jnp.einsum('rhd,khd->hrk', query_heads, key_heads)
    weights = jnp.where(key_live[None, None, :], jax.nn.silu(scores * head_size ** (-0.5)), 0.0).astype(jnp.bfloat16)
    mixed_rows = jnp.einsum('hrk,khd->rhd', weights.astype(jnp.float32), value_heads)
    return mixed_rows.reshape(row_count, feat_width)

def reference(item_table, item_ids, candidate_counts, domain_ids, history_lengths, history_keys, history_values, w_query, w_gate, w_out, attn_gain, expert_weights):
    flat_ids = item_ids.reshape(-1).astype(jnp.int32)
    embedded = jnp.take(item_table, flat_ids, axis=0)
    embed_float = embedded.astype(jnp.float32)
    normed = rms_scale(embed_float).astype(jnp.bfloat16)
    queries = jnp.dot(normed, w_query, preferred_element_type=jnp.float32).astype(jnp.bfloat16)
    gating = jax.nn.silu(jnp.dot(normed, w_gate, preferred_element_type=jnp.float32))
    user_queries = queries.reshape(USERS, SLOTS, D)

    def user_attention(packed):
        query_rows, key_rows, value_rows, length = packed
        key_blocks = key_rows.reshape(N_HIST, HIST_DEV, D)
        value_blocks = value_rows.reshape(N_HIST, HIST_DEV, D)
        offsets = jnp.arange(N_HIST, dtype=jnp.int32) * HIST_DEV

        def add_block(running, block):
            key_block, value_block, offset = block
            key_live = offset + jnp.arange(HIST_DEV, dtype=jnp.int32) < length
            return (running + attend_local(query_rows, key_block, value_block, key_live), None)
        attended, leftover = lax.scan(add_block, jnp.zeros((SLOTS, D), jnp.float32), (key_blocks, value_blocks, offsets))
        return attended
    attended = lax.map(user_attention, (user_queries, history_keys, history_values, history_lengths)).reshape(USERS * SLOTS, D)
    gated_rows = (rms_scale(attended) * attn_gain * gating).astype(jnp.bfloat16)
    item_state = (embed_float + jnp.dot(gated_rows, w_out, preferred_element_type=jnp.float32)).astype(jnp.bfloat16)

    def expert_chain(layer_set):
        current = item_state
        for layer_index in range(LAYERS):
            lifted = jnp.dot(current, layer_set[layer_index], preferred_element_type=jnp.float32)
            current = (current.astype(jnp.float32) + jax.nn.silu(lifted)).astype(jnp.bfloat16)
        return current
    expert_outputs = lax.map(expert_chain, expert_weights)
    flat_domains = domain_ids.reshape(-1).astype(jnp.int32)
    picked = expert_outputs[flat_domains, jnp.arange(USERS * SLOTS, dtype=jnp.int32)]
    live = (jnp.arange(SLOTS, dtype=jnp.int32)[None, :] < candidate_counts[:, None]).reshape(-1)
    result = jnp.where(live[:, None], picked, jnp.zeros_like(picked))
    return result.reshape(USERS, SLOTS, D)
```

```python
import functools

import jax
import jax.numpy as jnp
from jax import lax
from jax.experimental import pallas as pl
from jax.experimental.pallas import tpu as pltpu
from jax.sharding import PartitionSpec as P

H = 8
CHUNKS = 2
LAG = 3
norm_eps = 1e-05
MESH = pl.DeviceIdType.MESH


def rms_scale(matrix):
    return matrix * lax.rsqrt(jnp.mean(matrix * matrix, axis=-1, keepdims=True) + norm_eps)


def silu(value):
    half = value * 0.5
    return half + half * jnp.tanh(half)


def dot(left, right):
    return jnp.dot(left, right, preferred_element_type=jnp.float32)


def kernel(
    pairs,
    table,
    ids,
    counts,
    domains,
    lengths,
    keys,
    values,
    w_query,
    w_gate,
    w_out,
    gain,
    experts,
    out,
    rows,
    item_queries,
    key_buf,
    value_buf,
    query_w,
    gate_w,
    out_w,
    expert_w,
    id_buf,
    partial,
    pair_recv,
    z_send,
    z_recv,
    id_in,
    domain_in,
    gain_in,
    count_in,
    length_in,
    local_sem,
    table_zs,
    table_zr,
    table_ys,
    table_yr,
    table_ss,
    table_sr,
    id_zs,
    id_zr,
    id_ys,
    id_yr,
    expert_s,
    expert_r,
    sum_ys,
    sum_yr,
    sum_zs,
    sum_zr,
):
    me = lax.axis_index("hist")
    user = lax.axis_index("user")
    upper = lax.div(me, 2)
    lower = lax.rem(me, 2)
    slots = ids.shape[1]

    barrier = pltpu.get_barrier_semaphore()
    pl.semaphore_signal(
        barrier, inc=1, device_id={"hist": upper * 2 + (1 - lower)}, device_id_type=MESH
    )
    pl.semaphore_signal(barrier, inc=1, device_id={"user": 1 - user}, device_id_type=MESH)

    @pl.loop(1, pairs)
    def _(step):
        there = lax.rem(upper + step, pairs) * 2 + lower
        pl.semaphore_signal(barrier, inc=1, device_id={"hist": there}, device_id_type=MESH)

    shard, width = table.shape
    items = rows.shape[0]
    half = shard // 2
    key_count = key_buf.shape[0]
    layers = experts.shape[1]
    head = width // H

    def peer(step):
        return lax.rem(upper + step, pairs) * 2 + lower

    other = upper * 2 + (1 - lower)
    to_pair = {"hist": other}
    to_sibling = {"user": 1 - user}

    def remote(src, dst, send, recv, target):
        return pltpu.make_async_remote_copy(
            src_ref=src,
            dst_ref=dst,
            send_sem=send,
            recv_sem=recv,
            device_id=target,
            device_id_type=MESH,
        )

    def half_rows(owner, core):
        start = pl.multiple_of(owner * shard + core * half, half)
        return rows.at[pl.ds(start, half)]

    own_rows = rows.at[pl.ds(pl.multiple_of(me * shard, shard), shard)]
    loads = [
        pltpu.make_async_copy(table, own_rows, local_sem.at[0]),
        pltpu.make_async_copy(w_query, query_w, local_sem.at[1]),
        pltpu.make_async_copy(keys.at[0], key_buf, local_sem.at[2]),
        pltpu.make_async_copy(values.at[0], value_buf, local_sem.at[3]),
        pltpu.make_async_copy(w_gate, gate_w, local_sem.at[4]),
        pltpu.make_async_copy(w_out, out_w, local_sem.at[5]),
        pltpu.make_async_copy(experts.at[0], expert_w.at[user], local_sem.at[6]),
    ]
    id_load = pltpu.make_async_copy(ids, id_in, local_sem.at[7])
    id_load.start()
    for load in loads:
        load.start()

    small = [
        pltpu.make_async_copy(counts, count_in, local_sem.at[8]),
        pltpu.make_async_copy(lengths, length_in, local_sem.at[9]),
        pltpu.make_async_copy(domains, domain_in, local_sem.at[10]),
        pltpu.make_async_copy(gain, gain_in, local_sem.at[11]),
    ]
    for load in small:
        load.start()

    id_load.wait()
    id_tile = id_buf.at[lower, upper]
    id_tile[...] = jnp.zeros(id_tile.shape, jnp.int32)
    id_tile[0:1, 0:slots] = id_in[...]
    pl.semaphore_wait(barrier, pairs + 1)

    my_half = table.at[pl.ds(pl.multiple_of(user * half, half), half)]

    def id_z(step):
        return remote(id_tile, id_tile, id_zs.at[step], id_zr.at[step], {"hist": peer(step)})

    def id_z_arrival(step):
        source = lax.rem(upper - step + pairs, pairs)
        tile = id_buf.at[lower, source]
        return remote(tile, tile, id_zs.at[step], id_zr.at[step], {"hist": peer(step)})

    def table_z(step):
        return remote(
            my_half,
            half_rows(me, user),
            table_zs.at[step],
            table_zr.at[step],
            {"hist": peer(step)},
        )

    def source_at(step):
        return lax.rem(upper - step + pairs, pairs)

    def table_z_arrival(step):
        block = half_rows(source_at(step) * 2 + lower, user)
        return remote(
            block, block, table_zs.at[step], table_zr.at[step], {"hist": peer(step)}
        )

    def table_y(step, owner_low):
        block = half_rows(source_at(step) * 2 + owner_low, user)
        return remote(block, block, table_ys.at[step], table_yr.at[step], to_pair)

    def table_s(step, owner_low, core):
        block = half_rows(source_at(step) * 2 + owner_low, core)
        slot = 2 * step + jnp.where(owner_low == lower, 0, 1)
        return remote(block, block, table_ss.at[slot], table_sr.at[slot], to_sibling)

    @pl.loop(1, pairs)
    def _(step):
        table_z(step).start()

    table_y_first = remote(
        my_half, half_rows(me, user), table_ys.at[0], table_yr.at[0], to_pair
    )
    table_y_first.start()

    @pl.loop(1, pairs)
    def _(step):
        id_z(step).start()

    expert_copy = remote(experts.at[0], expert_w.at[user], expert_s, expert_r, to_sibling)
    expert_copy.start()

    def project(step):
        start = pl.multiple_of(source_at(step) * 2 * shard, 2 * shard)
        block = rows[pl.ds(start, 2 * shard), :].astype(jnp.float32)
        normed = rms_scale(block).astype(jnp.bfloat16)
        item_queries[pl.ds(start, 2 * shard), :] = dot(normed, query_w[...]).astype(jnp.bfloat16)

    table_y(0, 1 - lower).wait_recv()
    table_s(0, 1 - lower, user).start()
    loads[0].wait()
    loads[1].wait()

    @pl.loop(1, pairs)
    def _(step):
        table_z_arrival(step).wait_recv()
        table_y(step, lower).start()
        table_s(step, lower, user).start()

    @pl.loop(1, pairs)
    def _(step):
        id_z_arrival(step).wait_recv()

    id_y = remote(id_buf.at[lower], id_buf.at[lower], id_ys, id_yr, to_pair)
    id_y.start()

    @pl.loop(1, pairs)
    def _(step):
        table_y(step, 1 - lower).wait_recv()
        table_s(step, 1 - lower, user).start()
        previous = step - 1

        @pl.when(previous > 0)
        def _():
            table_s(previous, lower, 1 - user).wait_recv()

        table_s(previous, 1 - lower, 1 - user).wait_recv()
        project(previous)

    loads[2].wait()
    loads[3].wait()
    small[0].wait()
    small[1].wait()
    position = me * key_count + lax.broadcasted_iota(jnp.int32, (key_count, width), 0)
    value_buf[...] = jnp.where(position < length_in[...], value_buf[...], jnp.zeros((), jnp.bfloat16))
    table_s(pairs - 1, lower, 1 - user).wait_recv()
    table_s(pairs - 1, 1 - lower, 1 - user).wait_recv()
    project(pairs - 1)
    remote(
        id_buf.at[1 - lower], id_buf.at[1 - lower], id_ys, id_yr, to_pair
    ).wait_recv()

    lane_count = id_buf.shape[-1]
    eye = lax.broadcasted_iota(jnp.int32, (slots, lane_count), 0) == lax.broadcasted_iota(
        jnp.int32, (slots, lane_count), 1
    )

    def column(row):
        return jnp.sum(jnp.where(eye, row.astype(jnp.float32), 0.0), axis=1, keepdims=True)

    item_lane = lax.broadcasted_iota(jnp.int32, (slots, items), 1).astype(jnp.float32)

    def onehot(low, up):
        tile = id_buf[low, up]
        return jnp.where(item_lane == column(tile[0:1, :]), 1.0, 0.0).astype(jnp.bfloat16)

    turns = pairs * CHUNKS
    part = width // CHUNKS
    quads = pairs // 2
    quad = lax.div(upper, 2)
    side = lax.rem(upper, 2)

    def group_of(turn):
        return lax.rem(lax.div(turn, 2 * CHUNKS) + 1, quads)

    def near_of(turn):
        return lax.rem(lax.div(turn, CHUNKS), 2)

    def attend(turn):
        near = near_of(turn)
        chunk = lax.rem(turn, CHUNKS)
        target_side = near * side + (1 - near) * (1 - side)
        target = lax.rem(quad + group_of(turn), quads) * 2 + target_side
        chosen = jnp.concatenate([onehot(0, target), onehot(1, target)], axis=0)
        first = pl.multiple_of(chunk * part, part)
        queries = dot(chosen, item_queries[:, pl.ds(first, part)]).astype(jnp.bfloat16)
        for number in range(H // CHUNKS):
            cols = slice(number * head, (number + 1) * head)
            source = pl.ds(pl.multiple_of(first + number * head, head), head)
            scores = lax.dot_general(
                queries[:, cols],
                key_buf[:, source],
                (((1,), (1,)), ((), ())),
                preferred_element_type=jnp.float32,
            )
            halved = scores * (0.5 * head ** (-0.5))
            weights = (halved + halved * jnp.tanh(halved)).astype(jnp.bfloat16)
            mixed = dot(weights, value_buf[:, source]).astype(jnp.bfloat16)
            partial[turn, 0, :, cols] = mixed[:slots]
            partial[turn, 1, :, cols] = mixed[slots:]

    def sum_y(turn):
        return remote(
            partial.at[turn, 1 - lower],
            pair_recv.at[turn],
            sum_ys.at[turn],
            sum_yr.at[turn],
            to_pair,
        )

    def sum_z(turn):
        near = near_of(turn)
        across = lax.rem(quad + group_of(turn), quads) * 2 + side
        beside = quad * 2 + (1 - side)
        reached = near * across + (1 - near) * beside
        return remote(
            z_send.at[turn],
            z_recv.at[turn],
            sum_zs.at[turn],
            sum_zr.at[turn],
            {"hist": reached * 2 + lower},
        )

    def pair_sum(turn):
        sum_y(turn).wait_recv()
        return partial[turn, lower].astype(jnp.float32) + pair_recv[turn].astype(jnp.float32)

    def arrived_sum(turn):
        sum_z(turn).wait_recv()
        return z_recv[turn].astype(jnp.float32)

    def pass_on(turn):
        near = near_of(turn)

        @pl.when(near == 0)
        def _():
            z_send[turn] = pair_sum(turn).astype(jnp.bfloat16)

        @pl.when(near == 1)
        def _():
            z_send[turn] = (pair_sum(turn) + arrived_sum(turn - CHUNKS)).astype(jnp.bfloat16)

        sum_z(turn).start()

    @pl.loop(0, turns)
    def _(turn):
        attend(turn)
        sum_y(turn).start()

        @pl.when((turn >= LAG) & (turn < turns - CHUNKS + LAG))
        def _():
            pass_on(turn - LAG)

    if LAG > CHUNKS:

        @pl.loop(turns - LAG, turns - CHUNKS)
        def _(turn):
            pass_on(turn)

    loads[4].wait()
    loads[5].wait()
    small[2].wait()
    small[3].wait()
    embedded = dot(onehot(lower, upper), rows[...])
    normed = rms_scale(embedded).astype(jnp.bfloat16)
    gating = silu(dot(normed, gate_w[...])) * gain_in[...]

    sums = []
    for chunk in range(CHUNKS):
        last = turns - CHUNKS + chunk
        total = pair_sum(last) + arrived_sum(last - CHUNKS)

        def gather_sum(group, total, chunk=chunk):
            return total + arrived_sum((2 * group - 1) * CHUNKS + chunk)

        sums.append(lax.fori_loop(1, quads, gather_sum, total))
    attended = jnp.concatenate(sums, axis=1)
    gated = (rms_scale(attended) * gating).astype(jnp.bfloat16)
    state = (embedded + dot(gated, out_w[...])).astype(jnp.bfloat16)
    loads[6].wait()
    remote(
        experts.at[0], expert_w.at[1 - user], expert_s, expert_r, to_sibling
    ).wait_recv()

    results = []
    for expert in range(expert_w.shape[0]):
        current = state
        for layer in range(layers):
            lifted = dot(current, expert_w[expert, layer])
            current = (current.astype(jnp.float32) + silu(lifted)).astype(jnp.bfloat16)
        results.append(current)
    padded_domain = jnp.concatenate(
        [domain_in[...], jnp.zeros((1, lane_count - slots), jnp.int32)], axis=1
    )
    domain = column(padded_domain)
    picked = results[0].astype(jnp.float32)
    for expert in range(1, len(results)):
        picked = jnp.where(domain == expert, results[expert].astype(jnp.float32), picked)
    slot = me * slots + lax.broadcasted_iota(jnp.int32, (slots, 1), 0)
    out[0] = jnp.where(slot < count_in[...], picked, 0.0).astype(jnp.bfloat16)

    expert_copy.wait_send()
    table_y_first.wait_send()
    table_s(0, 1 - lower, user).wait_send()
    id_y.wait_send()

    @pl.loop(1, pairs)
    def _(step):
        id_z(step).wait_send()
        table_z(step).wait_send()
        table_y(step, lower).wait_send()
        table_s(step, lower, user).wait_send()
        table_s(step, 1 - lower, user).wait_send()

    @pl.loop(0, turns)
    def _(turn):
        sum_y(turn).wait_send()

    @pl.loop(0, turns - CHUNKS)
    def _(turn):
        sum_z(turn).wait_send()


def on_device(
    item_table,
    item_ids,
    candidate_counts,
    domain_ids,
    history_lengths,
    history_keys,
    history_values,
    w_query,
    w_gate,
    w_out,
    attn_gain,
    expert_weights,
):
    slots = item_ids.shape[1]
    shard, width = item_table.shape
    hist = lax.axis_size("hist")
    users = lax.axis_size("user")
    pairs = hist // 2
    turns = pairs * CHUNKS
    part = width // CHUNKS
    key_count = history_keys.shape[1]
    layers = expert_weights.shape[1]
    bf16 = jnp.bfloat16
    dma = pltpu.SemaphoreType.DMA
    anywhere = pl.BlockSpec(memory_space=pltpu.HBM)
    vmem = pl.BlockSpec(memory_space=pltpu.VMEM)
    lanes = 128 * ((slots + 127) // 128)
    return pl.pallas_call(
        functools.partial(kernel, pairs),
        out_shape=pltpu.VMEM((1, slots, width), bf16),
        in_specs=[anywhere] * 12,
        out_specs=vmem,
        scratch_shapes=[
            pltpu.VMEM((hist * shard, width), bf16),
            pltpu.VMEM((hist * shard, width), bf16),
            pltpu.VMEM((key_count, width), bf16),
            pltpu.VMEM((key_count, width), bf16),
            pltpu.VMEM(w_query.shape, bf16),
            pltpu.VMEM(w_gate.shape, bf16),
            pltpu.VMEM(w_out.shape, bf16),
            pltpu.VMEM((users, layers, width, width), bf16),
            pltpu.VMEM((2, pairs, 8, lanes), jnp.int32),
            pltpu.VMEM((turns, 2, slots, part), bf16),
            pltpu.VMEM((turns, slots, part), bf16),
            pltpu.VMEM((turns, slots, part), bf16),
            pltpu.VMEM((turns, slots, part), bf16),
            pltpu.VMEM((1, slots), jnp.int32),
            pltpu.VMEM((1, slots), jnp.int32),
            pltpu.VMEM((1, width), jnp.float32),
            pltpu.VMEM((1, 1), jnp.int32),
            pltpu.VMEM((1, 1), jnp.int32),
            dma((12,)),
            dma((pairs,)),
            dma((pairs,)),
            dma((pairs,)),
            dma((pairs,)),
            dma((2 * pairs,)),
            dma((2 * pairs,)),
            dma((pairs,)),
            dma((pairs,)),
            dma,
            dma,
            dma,
            dma,
            dma((turns,)),
            dma((turns,)),
            dma((turns,)),
            dma((turns,)),
        ],
        compiler_params=pltpu.CompilerParams(
            collective_id=0, has_side_effects=True, vmem_limit_bytes=60 * 1024 * 1024
        ),
    )(
        item_table,
        item_ids,
        candidate_counts.reshape(1, 1),
        domain_ids,
        history_lengths.reshape(1, 1),
        history_keys,
        history_values,
        w_query,
        w_gate,
        w_out,
        attn_gain.reshape(1, width),
        expert_weights,
    )


def solution(mesh):
    in_specs = (
        P("hist", None),
        P(("groups", "user"), "hist"),
        P(("groups", "user")),
        P(("groups", "user"), "hist"),
        P(("groups", "user")),
        P(("groups", "user"), "hist", None),
        P(("groups", "user"), "hist", None),
        P(),
        P(),
        P(),
        P(),
        P("user", None, None, None),
    )
    out_specs = P(("groups", "user"), "hist", None)
    return jax.shard_map(
        on_device, mesh=mesh, in_specs=in_specs, out_specs=out_specs, check_vma=False
    )
```

```python
import functools

import jax
import jax.numpy as jnp
from jax import lax
from jax.experimental import pallas as pl
from jax.experimental.pallas import tpu as pltpu
from jax.sharding import PartitionSpec as P

H = 8
CHUNKS = 2
LAG = 2
norm_eps = 1e-05
MESH = pl.DeviceIdType.MESH


def rms_scale(matrix):
    return matrix * lax.rsqrt(jnp.mean(matrix * matrix, axis=-1, keepdims=True) + norm_eps)


def silu(value):
    half = value * 0.5
    return half + half * jnp.tanh(half)


def dot(left, right):
    return jnp.dot(left, right, preferred_element_type=jnp.float32)


def kernel(
    pairs,
    table,
    ids,
    counts,
    domains,
    lengths,
    keys,
    values,
    w_query,
    w_gate,
    w_out,
    gain,
    experts,
    out,
    rows,
    item_queries,
    key_buf,
    value_buf,
    query_w,
    gate_w,
    out_w,
    expert_w,
    id_buf,
    partial,
    pair_recv,
    z_send,
    z_recv,
    id_in,
    domain_in,
    gain_in,
    count_in,
    length_in,
    local_sem,
    table_zs,
    table_zr,
    table_ys,
    table_yr,
    table_ss,
    table_sr,
    id_zs,
    id_zr,
    id_ys,
    id_yr,
    expert_s,
    expert_r,
    sum_ys,
    sum_yr,
    sum_zs,
    sum_zr,
):
    me = lax.axis_index("hist")
    user = lax.axis_index("user")
    upper = lax.div(me, 2)
    lower = lax.rem(me, 2)
    slots = ids.shape[1]

    barrier = pltpu.get_barrier_semaphore()
    pl.semaphore_signal(
        barrier, inc=1, device_id={"hist": upper * 2 + (1 - lower)}, device_id_type=MESH
    )
    pl.semaphore_signal(barrier, inc=1, device_id={"user": 1 - user}, device_id_type=MESH)

    @pl.loop(1, pairs)
    def _(step):
        there = lax.rem(upper + step, pairs) * 2 + lower
        pl.semaphore_signal(barrier, inc=1, device_id={"hist": there}, device_id_type=MESH)

    shard, width = table.shape
    items = rows.shape[0]
    half = shard // 2
    key_count = key_buf.shape[0]
    layers = experts.shape[1]
    head = width // H

    margin = jnp.minimum(upper, pairs - 1 - upper)
    toward = jnp.where(2 * upper < pairs, 1, -1)

    def near_peer(step):
        away = lax.div(step + 1, 2) * (2 * lax.rem(step, 2) - 1)
        return upper + jnp.where(step <= 2 * margin, away, toward * (step - margin))

    other = upper * 2 + (1 - lower)
    to_pair = {"hist": other}
    to_sibling = {"user": 1 - user}

    def remote(src, dst, send, recv, target):
        return pltpu.make_async_remote_copy(
            src_ref=src,
            dst_ref=dst,
            send_sem=send,
            recv_sem=recv,
            device_id=target,
            device_id_type=MESH,
        )

    def half_rows(owner, core):
        start = pl.multiple_of(owner * shard + core * half, half)
        return rows.at[pl.ds(start, half)]

    own_rows = rows.at[pl.ds(pl.multiple_of(me * shard, shard), shard)]
    loads = [
        pltpu.make_async_copy(table, own_rows, local_sem.at[0]),
        pltpu.make_async_copy(w_query, query_w, local_sem.at[1]),
        pltpu.make_async_copy(keys.at[0], key_buf, local_sem.at[2]),
        pltpu.make_async_copy(values.at[0], value_buf, local_sem.at[3]),
        pltpu.make_async_copy(w_gate, gate_w, local_sem.at[4]),
        pltpu.make_async_copy(w_out, out_w, local_sem.at[5]),
        pltpu.make_async_copy(experts.at[0], expert_w.at[user], local_sem.at[6]),
    ]
    id_load = pltpu.make_async_copy(ids, id_in, local_sem.at[7])
    id_load.start()
    loads[0].start()
    loads[1].start()

    small = [
        pltpu.make_async_copy(counts, count_in, local_sem.at[8]),
        pltpu.make_async_copy(lengths, length_in, local_sem.at[9]),
        pltpu.make_async_copy(domains, domain_in, local_sem.at[10]),
        pltpu.make_async_copy(gain, gain_in, local_sem.at[11]),
    ]
    id_load.wait()
    id_tile = id_buf.at[lower, upper]
    id_tile[...] = jnp.zeros(id_tile.shape, jnp.int32)
    id_tile[0:1, 0:slots] = id_in[...]
    pl.semaphore_wait(barrier, pairs + 1)

    loads[0].wait()
    my_half = half_rows(me, user)

    def id_z(source, there):
        tile = id_buf.at[lower, source]
        return remote(tile, tile, id_zs, id_zr.at[source], {"hist": there * 2 + lower})

    def table_z(source, there):
        block = half_rows(source * 2 + lower, user)
        return remote(
            block, block, table_zs, table_zr.at[source], {"hist": there * 2 + lower}
        )

    def table_y(source, owner_low):
        block = half_rows(source * 2 + owner_low, user)
        return remote(block, block, table_ys, table_yr.at[source], to_pair)

    def table_s(source, owner_low, core):
        block = half_rows(source * 2 + owner_low, core)
        slot = 2 * source + jnp.where(owner_low == lower, 0, 1)
        return remote(block, block, table_ss, table_sr.at[slot], to_sibling)

    table_y(upper, lower).start()

    @pl.loop(1, pairs)
    def _(step):
        table_z(upper, near_peer(step)).start()

    @pl.loop(1, pairs)
    def _(step):
        id_z(upper, near_peer(step)).start()

    loads[2].start()
    loads[3].start()
    for load in small:
        load.start()

    def project(source):
        start = pl.multiple_of(source * 2 * shard, 2 * shard)
        block = rows[pl.ds(start, 2 * shard), :].astype(jnp.float32)
        normed = rms_scale(block).astype(jnp.bfloat16)
        item_queries[pl.ds(start, 2 * shard), :] = dot(normed, query_w[...]).astype(jnp.bfloat16)

    def forward(step):
        source = near_peer(step)
        table_z(source, upper).wait_recv()
        table_y(source, lower).start()
        table_s(source, lower, user).start()

    def finish(step):
        source = near_peer(step)
        table_y(source, 1 - lower).wait_recv()
        table_s(source, 1 - lower, user).start()

    def complete(source):
        table_s(source, lower, 1 - user).wait_recv()
        table_s(source, 1 - lower, 1 - user).wait_recv()

    table_y(upper, 1 - lower).wait_recv()
    table_s(upper, 1 - lower, user).start()
    loads[1].wait()

    @pl.loop(1, pairs)
    def _(step):
        forward(step)

    loads[2].wait()
    loads[3].wait()
    small[0].wait()
    small[1].wait()
    position = me * key_count + lax.broadcasted_iota(jnp.int32, (key_count, width), 0)
    value_buf[...] = jnp.where(
        position < length_in[...], value_buf[...], jnp.zeros((), jnp.bfloat16)
    )

    @pl.loop(1, pairs)
    def _(step):
        id_z(near_peer(step), upper).wait_recv()

    id_y = remote(id_buf.at[lower], id_buf.at[lower], id_ys, id_yr, to_pair)
    id_y.start()
    finish(1)
    table_s(upper, 1 - lower, 1 - user).wait_recv()
    project(upper)

    @pl.loop(1, pairs)
    def _(step):
        @pl.when(step < pairs - 1)
        def _():
            finish(step + 1)

        complete(near_peer(step))
        project(near_peer(step))

    remote(
        id_buf.at[1 - lower], id_buf.at[1 - lower], id_ys, id_yr, to_pair
    ).wait_recv()
    loads[4].start()
    loads[5].start()
    loads[6].start()
    expert_copy = remote(experts.at[0], expert_w.at[user], expert_s, expert_r, to_sibling)
    expert_copy.start()

    lane_count = id_buf.shape[-1]
    eye = lax.broadcasted_iota(jnp.int32, (slots, lane_count), 0) == lax.broadcasted_iota(
        jnp.int32, (slots, lane_count), 1
    )

    def column(row):
        return jnp.sum(jnp.where(eye, row.astype(jnp.float32), 0.0), axis=1, keepdims=True)

    item_lane = lax.broadcasted_iota(jnp.int32, (slots, items), 1).astype(jnp.float32)

    def onehot(low, up):
        tile = id_buf[low, up]
        return jnp.where(item_lane == column(tile[0:1, :]), 1.0, 0.0).astype(jnp.bfloat16)

    turns = pairs * CHUNKS
    part = width // CHUNKS
    quads = pairs // 2
    quad = lax.div(upper, 2)
    side = lax.rem(upper, 2)

    early = quads * CHUNKS

    def group_of(turn):
        return lax.rem(lax.rem(lax.div(turn, CHUNKS), quads) + 1, quads)

    def near_of(turn):
        return lax.div(turn, early)

    def attend(turn):
        near = near_of(turn)
        chunk = lax.rem(turn, CHUNKS)
        target_side = near * side + (1 - near) * (1 - side)
        target = lax.rem(quad + group_of(turn), quads) * 2 + target_side
        chosen = jnp.concatenate([onehot(0, target), onehot(1, target)], axis=0)
        first = pl.multiple_of(chunk * part, part)
        queries = dot(chosen, item_queries[:, pl.ds(first, part)]).astype(jnp.bfloat16)
        for number in range(H // CHUNKS):
            cols = slice(number * head, (number + 1) * head)
            source = pl.ds(pl.multiple_of(first + number * head, head), head)
            scores = lax.dot_general(
                queries[:, cols],
                key_buf[:, source],
                (((1,), (1,)), ((), ())),
                preferred_element_type=jnp.float32,
            )
            halved = scores * (0.5 * head ** (-0.5))
            weights = (halved + halved * jnp.tanh(halved)).astype(jnp.bfloat16)
            mixed = dot(weights, value_buf[:, source]).astype(jnp.bfloat16)
            partial[turn, 0, :, cols] = mixed[:slots]
            partial[turn, 1, :, cols] = mixed[slots:]

    def sum_y(turn):
        return remote(
            partial.at[turn, 1 - lower],
            pair_recv.at[turn],
            sum_ys,
            sum_yr.at[turn],
            to_pair,
        )

    def sum_z(turn):
        near = near_of(turn)
        across = lax.rem(quad + group_of(turn), quads) * 2 + side
        beside = quad * 2 + (1 - side)
        reached = near * across + (1 - near) * beside
        return remote(
            z_send.at[turn],
            z_recv.at[turn],
            sum_zs,
            sum_zr.at[turn],
            {"hist": reached * 2 + lower},
        )

    def pair_sum(turn):
        sum_y(turn).wait_recv()
        return partial[turn, lower].astype(jnp.float32) + pair_recv[turn].astype(jnp.float32)

    def arrived_sum(turn):
        sum_z(turn).wait_recv()
        return z_recv[turn].astype(jnp.float32)

    def pass_on(turn):
        near = near_of(turn)

        @pl.when(near == 0)
        def _():
            z_send[turn] = pair_sum(turn).astype(jnp.bfloat16)

        @pl.when(near == 1)
        def _():
            z_send[turn] = (pair_sum(turn) + arrived_sum(turn - early)).astype(jnp.bfloat16)

        sum_z(turn).start()

    @pl.loop(0, turns)
    def _(turn):
        attend(turn)
        sum_y(turn).start()

        @pl.when((turn >= LAG) & (turn < turns - CHUNKS + LAG))
        def _():
            pass_on(turn - LAG)

    if LAG > CHUNKS:

        @pl.loop(turns - LAG, turns - CHUNKS)
        def _(turn):
            pass_on(turn)

    loads[4].wait()
    loads[5].wait()
    small[2].wait()
    small[3].wait()
    embedded = dot(onehot(lower, upper), rows[...])
    normed = rms_scale(embedded).astype(jnp.bfloat16)
    gating = silu(dot(normed, gate_w[...])) * gain_in[...]

    expert_copy.wait_send()
    id_y.wait_send()

    def sent(count, sem):
        block = rows.at[pl.ds(0, count * half)]
        remote(block, block, sem, table_yr.at[0], to_pair).wait_send()

    sent(pairs - 1, table_zs)
    sent(pairs, table_ys)
    sent(2 * pairs - 1, table_ss)
    tiles = id_buf.at[0, pl.ds(0, pairs - 1)]
    remote(tiles, tiles, id_zs, id_yr, to_pair).wait_send()

    sums = []
    for chunk in range(CHUNKS):
        last = turns - CHUNKS + chunk
        total = pair_sum(last) + arrived_sum(last - early)

        def gather_sum(group, total, chunk=chunk):
            return total + arrived_sum((quads + group - 1) * CHUNKS + chunk)

        sums.append(lax.fori_loop(1, quads, gather_sum, total))
    attended = jnp.concatenate(sums, axis=1)
    gated = (rms_scale(attended) * gating).astype(jnp.bfloat16)
    state = (embedded + dot(gated, out_w[...])).astype(jnp.bfloat16)
    loads[6].wait()
    remote(
        experts.at[0], expert_w.at[1 - user], expert_s, expert_r, to_sibling
    ).wait_recv()

    results = []
    for expert in range(expert_w.shape[0]):
        current = state
        for layer in range(layers):
            lifted = dot(current, expert_w[expert, layer])
            current = (current.astype(jnp.float32) + silu(lifted)).astype(jnp.bfloat16)
        results.append(current)
    padded_domain = jnp.concatenate(
        [domain_in[...], jnp.zeros((1, lane_count - slots), jnp.int32)], axis=1
    )
    domain = column(padded_domain)
    picked = results[0].astype(jnp.float32)
    for expert in range(1, len(results)):
        picked = jnp.where(domain == expert, results[expert].astype(jnp.float32), picked)
    slot = me * slots + lax.broadcasted_iota(jnp.int32, (slots, 1), 0)
    out[0] = jnp.where(slot < count_in[...], picked, 0.0).astype(jnp.bfloat16)

    remote(pair_recv, pair_recv, sum_ys, sum_yr.at[0], to_pair).wait_send()
    sent_z = z_recv.at[pl.ds(0, turns - CHUNKS)]
    remote(sent_z, sent_z, sum_zs, sum_zr.at[0], to_pair).wait_send()


def on_device(
    item_table,
    item_ids,
    candidate_counts,
    domain_ids,
    history_lengths,
    history_keys,
    history_values,
    w_query,
    w_gate,
    w_out,
    attn_gain,
    expert_weights,
):
    slots = item_ids.shape[1]
    shard, width = item_table.shape
    hist = lax.axis_size("hist")
    users = lax.axis_size("user")
    pairs = hist // 2
    turns = pairs * CHUNKS
    part = width // CHUNKS
    key_count = history_keys.shape[1]
    layers = expert_weights.shape[1]
    bf16 = jnp.bfloat16
    dma = pltpu.SemaphoreType.DMA
    anywhere = pl.BlockSpec(memory_space=pltpu.HBM)
    vmem = pl.BlockSpec(memory_space=pltpu.VMEM)
    lanes = 128 * ((slots + 127) // 128)
    return pl.pallas_call(
        functools.partial(kernel, pairs),
        out_shape=pltpu.VMEM((1, slots, width), bf16),
        in_specs=[anywhere] * 12,
        out_specs=vmem,
        scratch_shapes=[
            pltpu.VMEM((hist * shard, width), bf16),
            pltpu.VMEM((hist * shard, width), bf16),
            pltpu.VMEM((key_count, width), bf16),
            pltpu.VMEM((key_count, width), bf16),
            pltpu.VMEM(w_query.shape, bf16),
            pltpu.VMEM(w_gate.shape, bf16),
            pltpu.VMEM(w_out.shape, bf16),
            pltpu.VMEM((users, layers, width, width), bf16),
            pltpu.VMEM((2, pairs, 8, lanes), jnp.int32),
            pltpu.VMEM((turns, 2, slots, part), bf16),
            pltpu.VMEM((turns, slots, part), bf16),
            pltpu.VMEM((turns, slots, part), bf16),
            pltpu.VMEM((turns, slots, part), bf16),
            pltpu.VMEM((1, slots), jnp.int32),
            pltpu.VMEM((1, slots), jnp.int32),
            pltpu.VMEM((1, width), jnp.float32),
            pltpu.VMEM((1, 1), jnp.int32),
            pltpu.VMEM((1, 1), jnp.int32),
            dma((12,)),
            dma,
            dma((pairs,)),
            dma,
            dma((pairs,)),
            dma,
            dma((2 * pairs,)),
            dma,
            dma((pairs,)),
            dma,
            dma,
            dma,
            dma,
            dma,
            dma((turns,)),
            dma,
            dma((turns,)),
        ],
        compiler_params=pltpu.CompilerParams(
            collective_id=0, has_side_effects=True, vmem_limit_bytes=60 * 1024 * 1024
        ),
    )(
        item_table,
        item_ids,
        candidate_counts.reshape(1, 1),
        domain_ids,
        history_lengths.reshape(1, 1),
        history_keys,
        history_values,
        w_query,
        w_gate,
        w_out,
        attn_gain.reshape(1, width),
        expert_weights,
    )


def solution(mesh):
    in_specs = (
        P("hist", None),
        P(("groups", "user"), "hist"),
        P(("groups", "user")),
        P(("groups", "user"), "hist"),
        P(("groups", "user")),
        P(("groups", "user"), "hist", None),
        P(("groups", "user"), "hist", None),
        P(),
        P(),
        P(),
        P(),
        P("user", None, None, None),
    )
    out_specs = P(("groups", "user"), "hist", None)
    return jax.shard_map(
        on_device, mesh=mesh, in_specs=in_specs, out_specs=out_specs, check_vma=False
    )
```
